32 devices in a mesh: dp: 2 (over x), fsdp: 16 (over z, y, core).
Axes of the slice: x: 2, y: 2, z: 4, core: 2. Of those that a mesh axis runs over, the one named last changes fastest.
Arguments:
- activations: bfloat16 [2, 32, 128, 768], P(None, ('dp', 'fsdp')), may hold values from -6 to 6
- pair_repr: bfloat16 [2, 32, 128, 128, 256], P(None, ('dp', 'fsdp')), may hold values from -6 to 6
- cotangent: bfloat16 [2, 32, 128, 768], P(None, ('dp', 'fsdp')), may hold values from -6 to 6
- buckets: int32 [2, 32], P(None, ('dp', 'fsdp')), may hold values from 32 to 128, as said below
- pad_mask: int32 [2, 32, 128], P(None, ('dp', 'fsdp')), may hold values 0 or 1
- cath_ids: int32 [2, 32], P(None, ('dp', 'fsdp')), may hold values from 0 to 1023
- time_bins: int32 [2, 32], P(None, ('dp', 'fsdp')), may hold values from 0 to 999
- cath_table: bfloat16 [1024, 768], P(None, 'fsdp'), may hold values from -4.1875 to 4.1875
- time_table: bfloat16 [1000, 768], P(None, 'fsdp'), may hold values from -4.1875 to 4.1875
- cond_attn: bfloat16 [768, 2304], P('fsdp'), may hold values from -0.21875 to 0.21875
- cond_ffn: bfloat16 [768, 2304], P('fsdp'), may hold values from -0.21875 to 0.21875
- norm_attn: bfloat16 [768], P('fsdp'), may hold values from 0.5 to 1.5
- norm_ffn: bfloat16 [768], P('fsdp'), may hold values from 0.5 to 1.5
- pair_gain: bfloat16 [256], P('fsdp'), may hold values from 0.5 to 1.5
- qkv_weight: bfloat16 [768, 2304], P('fsdp'), may hold values from -0.21875 to 0.21875
- out_weight: bfloat16 [768, 768], P('fsdp'), may hold values from -0.875 to 0.875
- pair_weight: bfloat16 [256, 12], P('fsdp'), may hold values from -0.375 to 0.375
- gateup_weight: bfloat16 [768, 6144], P('fsdp'), may hold values from -0.21875 to 0.21875
- down_weight: bfloat16 [3072, 768], P('fsdp'), may hold values from -0.109375 to 0.109375
Outputs:
- block_out: bfloat16 [2, 32, 128, 768], P(None, ('dp', 'fsdp'))
- grad_input: bfloat16 [2, 32, 128, 768], P(None, ('dp', 'fsdp'))
- grad_pair: bfloat16 [2, 32, 128, 128, 256], P(None, ('dp', 'fsdp'))
- grad_cath: float32 [1024, 768], P(None, 'fsdp')
- grad_time: float32 [1000, 768], P(None, 'fsdp')
- grad_cond_attn: float32 [768, 2304], P('fsdp')
- grad_cond_ffn: float32 [768, 2304], P('fsdp')
- grad_norm_attn: float32 [768], P('fsdp')
- grad_norm_ffn: float32 [768], P('fsdp')
- grad_pair_gain: float32 [256], P('fsdp')
- grad_qkv_weight: float32 [768, 2304], P('fsdp')
- grad_out_weight: float32 [768, 768], P('fsdp')
- grad_pair_weight: float32 [256, 12], P('fsdp')
- grad_gateup_weight: float32 [768, 6144], P('fsdp')
- grad_down_weight: float32 [3072, 768], P('fsdp')
The draws below stay inside these ranges and needn't reach their ends.
Inputs may be any that keep to these rules, and one draw needn't show every extreme that they name: `buckets`: each bucket size is 128, 64 or 32.
All inputs are finite; a program needn't handle non-finite values. No bound on the sum of `pad_mask` on one device may be relied on, other than what follows from the above.
Results may differ from the reference program's by a relative error of at most 0.024.
Values may be sent and summed in bfloat16 or wider, within the bound.
No kernel may reach another device: no remote copies, remote signals or barrier semaphores. Data moves between devices by JAX's collectives and lax.ppermute only.
A program may use at most 256 MiB of HBM per device.

```python
import math
import jax
import jax.numpy as jnp
from jax import lax

D = 768
HEADS = 12
CP = 256
FF = 3072
NCATH = 1024
NTIME = 1000
LP = 128
MB = 2
CHAINS = 32


def draw_buckets(key, part):
    levels = jax.random.randint(key, (MB, CHAINS), 0, 3)
    sizes = jnp.where(levels == 0, LP, jnp.where(levels == 1, LP // 2, LP // 4)).astype(jnp.int32)
    sizes = sizes.at[0, 0].set(LP)
    sizes = sizes.at[0, 1].set(LP // 4)
    return sizes


def touch_ends(values, rng, smallest, largest):
    longest = values.shape.index(max(values.shape))
    spots = []
    for shift in (0, 1):
        where = [jax.random.randint(jax.random.fold_in(rng, axis), (), 0, length) for axis, length in enumerate(values.shape)]
        where[longest] = (where[longest] + shift) % values.shape[longest]
        spots.append(tuple(where))
    return values.at[spots[0]].set(smallest).at[spots[1]].set(largest)


def level_of(key, shape, pieces, low, largest):
    factor_of = 1.0
    for dim, parts in pieces:
        draws = jax.random.uniform(jax.random.fold_in(jax.random.fold_in(key, 6), dim), (parts,), jnp.float32, low / len(pieces), largest / len(pieces))
        factor_of = factor_of * jnp.repeat(jnp.exp(draws), shape[dim] // parts).reshape((-1,) + (1,) * (len(shape) - 1 - dim))
    return factor_of


def normal_values(rng, dims, width, reach, shards=(), kind=jnp.bfloat16):
    loudness = level_of(rng, dims, shards, -0.22, 0.18) if shards else 1.0
    values = jax.random.normal(rng, dims, jnp.float32) * width * loudness
    return jnp.minimum(jnp.maximum(values, -reach), reach).astype(kind)


def setup_inputs(seed: int = 0) -> dict:
    seeds = jax.random.split(jax.random.key(seed), 20)
    activations = normal_values(seeds[0], (MB, CHAINS, LP, D), 1.0, 6.0, ((1, 32),))
    pair_repr = normal_values(seeds[1], (MB, CHAINS, LP, LP, CP), 1.0, 6.0, ((1, 32),))
    cotangent = normal_values(seeds[2], (MB, CHAINS, LP, D), 1.0, 6.0, ((1, 32),))
    buckets = draw_buckets(jax.random.fold_in(seeds[19], 71), 0)
    pad_mask = touch_ends((jax.random.randint(seeds[4], (MB, CHAINS, LP), 0, 8) < 7).astype(jnp.int32), jax.random.fold_in(seeds[4], 1), 0, 1)
    cath_ids = touch_ends(jax.random.randint(seeds[5], (MB, CHAINS), 0, NCATH), jax.random.fold_in(seeds[5], 1), 0, NCATH - 1).astype(jnp.int32)
    time_bins = touch_ends(jax.random.randint(seeds[6], (MB, CHAINS), 0, NTIME), jax.random.fold_in(seeds[6], 1), 0, NTIME - 1).astype(jnp.int32)
    cath_table = normal_values(seeds[7], (NCATH, D), 0.7, 4.1875, ((1, 16),))
    time_table = normal_values(seeds[8], (NTIME, D), 0.7, 4.1875, ((1, 16),))
    cond_attn = normal_values(seeds[9], (D, 3 * D), D ** -0.5, 0.21875, ((0, 16),))
    cond_ffn = normal_values(seeds[10], (D, 3 * D), D ** -0.5, 0.21875, ((0, 16),))
    norm_attn = jnp.clip(1.0 + 0.1 * jax.random.normal(seeds[11], (D,), jnp.float32), 0.5, 1.5).astype(jnp.bfloat16)
    norm_ffn = jnp.clip(1.0 + 0.1 * jax.random.normal(seeds[12], (D,), jnp.float32), 0.5, 1.5).astype(jnp.bfloat16)
    pair_gain = jnp.clip(1.0 + 0.1 * jax.random.normal(seeds[13], (CP,), jnp.float32), 0.5, 1.5).astype(jnp.bfloat16)
    qkv_weight = normal_values(seeds[14], (D, 3 * D), D ** -0.5, 0.21875, ((0, 16),))
    out_weight = normal_values(seeds[15], (D, D), (D // 16) ** -0.5, 0.875, ((0, 16),))
    pair_weight = normal_values(seeds[16], (CP, HEADS), CP ** -0.5, 0.375, ((0, 16),))
    gateup_weight = normal_values(seeds[17], (D, 2 * FF), D ** -0.5, 0.21875, ((0, 16),))
    down_weight = normal_values(seeds[18], (FF, D), FF ** -0.5, 0.109375, ((0, 16),))
    return dict(activations=activations, pair_repr=pair_repr, cotangent=cotangent, buckets=buckets, pad_mask=pad_mask, cath_ids=cath_ids, time_bins=time_bins, cath_table=cath_table, time_table=time_table, cond_attn=cond_attn, cond_ffn=cond_ffn, norm_attn=norm_attn, norm_ffn=norm_ffn, pair_gain=pair_gain, qkv_weight=qkv_weight, out_weight=out_weight, pair_weight=pair_weight, gateup_weight=gateup_weight, down_weight=down_weight)


@jax.custom_vjp
def low(v):
    return lax.optimization_barrier(v.astype(jnp.bfloat16)).astype(jnp.float32)

@jax.custom_vjp
def low_back(v):
    return v

def low_keep(v):
    return (low(v), None)

def low_pass(kept, grad):
    return (grad,)

def back_keep(v):
    return (v, None)

def back_low(kept, grad):
    return (low(grad),)
low.defvjp(low_keep, low_pass)
low_back.defvjp(back_keep, back_low)

def normed_rows(values):
    center = values - lax.optimization_barrier(jnp.mean(values, axis=-1, keepdims=True))
    return center * lax.rsqrt(lax.optimization_barrier(jnp.mean(center * center, axis=-1, keepdims=True)) + 1e-05)

def chain_layer(params, chain_act, chain_pair, live_keys, cath_id, time_bin):
    cath_table, time_table, cond_attn, cond_ffn, norm_attn, norm_ffn, pair_gain, qkv_weight, out_weight, pair_weight, gateup_weight, down_weight = params
    highest = lax.Precision.HIGHEST
    model_width = chain_act.shape[-1]
    length = chain_act.shape[0]
    head_count = pair_weight.shape[1]
    head_size = model_width // head_count
    hidden_width = down_weight.shape[0]
    score_scale = 1.0 / math.sqrt(head_size)
    cond_raw = cath_table[cath_id] + time_table[time_bin]
    cond_act = low(jax.nn.silu(cond_raw))
    mod_attn = jnp.dot(cond_act, cond_attn, precision=highest)
    mod_ffn = jnp.dot(cond_act, cond_ffn, precision=highest)
    row_live = live_keys.astype(jnp.float32)[:, None]
    normed_attn = low(normed_rows(chain_act) * norm_attn * (1.0 + mod_attn[model_width:2 * model_width]) + mod_attn[:model_width])
    projected = low(low_back(jnp.dot(normed_attn, qkv_weight, precision=highest)))
    query_heads = projected[:, :model_width].reshape(length, head_count, head_size)
    key_heads = projected[:, model_width:2 * model_width].reshape(length, head_count, head_size)
    value_heads = projected[:, 2 * model_width:].reshape(length, head_count, head_size)
    pair_in = low(normed_rows(chain_pair) * pair_gain)
    pair_bias = low_back(jnp.einsum('ijc,ch->hij', pair_in, pair_weight, precision=highest))
    scores = low_back(jnp.einsum('ihd,jhd->hij', query_heads, key_heads, precision=highest) * score_scale + pair_bias)
    scores = jnp.where(live_keys[None, None, :], scores, -1000000000.0)
    attn_probs = jax.nn.softmax(scores, axis=-1)
    attn_mixed = low(low_back(jnp.einsum('hij,jhd->ihd', low(attn_probs), value_heads, precision=highest).reshape(length, model_width)))
    branch_attn = low_back(jnp.dot(attn_mixed, out_weight, precision=highest))
    after_attn = chain_act + mod_attn[2 * model_width:] * row_live * branch_attn
    normed_ffn = low(normed_rows(after_attn) * norm_ffn * (1.0 + mod_ffn[model_width:2 * model_width]) + mod_ffn[:model_width])
    gate_up = low(low_back(jnp.dot(normed_ffn, gateup_weight, precision=highest)))
    hidden = low(jax.nn.silu(gate_up[:, :hidden_width]) * gate_up[:, hidden_width:])
    branch_ffn = low_back(jnp.dot(hidden, down_weight, precision=highest))
    return after_attn + mod_ffn[2 * model_width:] * row_live * branch_ffn

def reference(activations, pair_repr, cotangent, buckets, pad_mask, cath_ids, time_bins, cath_table, time_table, cond_attn, cond_ffn, norm_attn, norm_ffn, pair_gain, qkv_weight, out_weight, pair_weight, gateup_weight, down_weight):
    params = tuple((weight.astype(jnp.float32) for weight in (cath_table, time_table, cond_attn, cond_ffn, norm_attn, norm_ffn, pair_gain, qkv_weight, out_weight, pair_weight, gateup_weight, down_weight)))
    positions = jnp.arange(LP, dtype=jnp.int32)
    live_keys = (positions[None, None, :] < buckets[:, :, None]) & ((pad_mask == 1) | (positions[None, None, :] == 0))
    groups = MB * CHAINS // 4

    def regroup(array):
        return array.reshape((groups, 4) + array.shape[2:])
    chain_items = (regroup(activations), regroup(pair_repr), regroup(cotangent), regroup(live_keys), regroup(cath_ids), regroup(time_bins))

    def group_step(totals, batch_item):
        group_act, group_pair, group_cot, group_live, group_cath, group_time = batch_item

        def forward(weights, inputs, pairs):
            return jax.vmap(chain_layer, in_axes=(None, 0, 0, 0, 0, 0))(weights, inputs, pairs, group_live, group_cath, group_time)
        outputs, pullback = jax.vjp(forward, params, group_act.astype(jnp.float32), group_pair.astype(jnp.float32))
        grad_params, grad_act, grad_pair = pullback(group_cot.astype(jnp.float32))
        totals = jax.tree.map(jnp.add, totals, grad_params)
        return (totals, (outputs.astype(jnp.bfloat16), grad_act.astype(jnp.bfloat16), grad_pair.astype(jnp.bfloat16)))
    zero_grads = tuple((jnp.zeros(weight.shape, jnp.float32) for weight in params))
    grad_sums, (outputs, grad_act, grad_pair) = lax.scan(group_step, zero_grads, chain_items)
    return (outputs.reshape(activations.shape), grad_act.reshape(activations.shape), grad_pair.reshape(pair_repr.shape), grad_sums[0], grad_sums[1], grad_sums[2], grad_sums[3], grad_sums[4], grad_sums[5], grad_sums[6], grad_sums[7], grad_sums[8], grad_sums[9], grad_sums[10], grad_sums[11])
```

```python
import math
import jax
import jax.numpy as jnp
from jax import lax
from jax.experimental import pallas as pl
from jax.experimental.pallas import tpu as pltpu
from jax.sharding import PartitionSpec as P

F32 = jnp.float32
BF16 = jnp.bfloat16
EPS = 1e-05
SLOTS = 16
EVERY = ("dp", "fsdp")
VMEM_BYTES = 48 * 1024 * 1024


def dot(a, b, a_dim, b_dim):
    return lax.dot_general(a, b, (((a_dim,), (b_dim,)), ((), ())), preferred_element_type=F32)


def pair_forward_kernel(pair_ref, center_ref, weight_ref, square_ref, out_ref):
    rows, length, channels = pair_ref.shape[1:]
    group = length // SLOTS
    slot = lax.broadcasted_iota(jnp.int32, (group, SLOTS, length), 1)
    for start in range(0, rows, group):
        block = pair_ref[0, start : start + group].reshape(group * length, channels)
        centered = dot(block, center_ref[...], 1, 0)
        low = centered.astype(BF16)
        square = (centered * centered).astype(BF16)
        raw = dot(low, weight_ref[...], 1, 0) + dot(square, square_ref[...], 1, 0)
        packed = raw[:length]
        for k in range(1, group):
            packed = packed + pltpu.roll(raw[k * length : (k + 1) * length], SLOTS * k, 1)
        turned = packed.T.reshape(group, SLOTS, length)
        inverse = lax.rsqrt(turned[:, SLOTS - 1 :, :] + EPS)
        out_ref[0, start : start + group] = jnp.where(slot == SLOTS - 1, inverse, turned * inverse)


def pair_forward(pair, center, weight, square):
    count, length, _, channels = pair.shape
    rows = 16
    return pl.pallas_call(
        pair_forward_kernel,
        grid=(count, length // rows),
        in_specs=[
            pl.BlockSpec((1, rows, length, channels), lambda n, i: (n, i, 0, 0)),
            pl.BlockSpec(center.shape, lambda n, i: (0, 0)),
            pl.BlockSpec(weight.shape, lambda n, i: (0, 0)),
            pl.BlockSpec(square.shape, lambda n, i: (0, 0)),
        ],
        out_specs=pl.BlockSpec((1, rows, SLOTS, length), lambda n, i: (n, i, 0, 0)),
        out_shape=jax.ShapeDtypeStruct((count, length, SLOTS, length), F32),
        compiler_params=pltpu.CompilerParams(vmem_limit_bytes=VMEM_BYTES),
        cost_estimate=pl.CostEstimate(
            flops=2 * pair.size * 3 * 256, bytes_accessed=2 * pair.size, transcendentals=0
        ),
        name="pair_forward",
    )(pair, center, weight, square)


def pair_backward_kernel(heads, pair_ref, grad_ref, stat_ref, center_ref, spread_ref, out_ref, sum_ref):
    rows, length, channels = pair_ref.shape[1:]
    group = length // SLOTS

    @pl.when((pl.program_id(0) == 0) & (pl.program_id(1) == 0))
    def _():
        sum_ref[...] = jnp.zeros_like(sum_ref)

    slot = lax.broadcasted_iota(jnp.int32, (group, SLOTS, length), 1)
    lane_slot = lax.broadcasted_iota(jnp.int32, (length, length), 1) // SLOTS
    total = jnp.zeros(sum_ref.shape, F32)
    for start in range(0, rows, group):
        block = pair_ref[0, start : start + group].reshape(group * length, channels)
        centered = dot(block, center_ref[...], 1, 0)
        low = centered.astype(BF16)
        grads = jnp.where(slot < heads, grad_ref[0, start : start + group], 0.0)
        stats = stat_ref[0, start : start + group]
        inverse = stats[:, SLOTS - 1 :, :]
        inner = jnp.sum(jnp.where(slot < heads, grads * stats, 0.0), axis=1, keepdims=True)
        slope = inner * inverse * inverse * (-1.0 / channels)
        slope_high = slope.astype(BF16).astype(F32)
        left = jnp.where(slot < heads, grads * inverse, 0.0)
        left = jnp.where(slot == heads, slope_high, left)
        left = jnp.where(slot == heads + 1, slope - slope_high, left)
        left = left.reshape(group * SLOTS, length)
        left_low = left.astype(BF16)
        turned = left.T.astype(BF16)
        for k in range(group):
            part = jnp.where(lane_slot == k, turned, jnp.zeros_like(turned))
            spread = dot(part, spread_ref[...], 1, 0)
            here = slice(k * length, (k + 1) * length)
            out_ref[0, start + k] = (spread[:, :channels] + centered[here] * spread[:, channels:]).astype(BF16)
            total = total + dot(left_low[k * SLOTS : (k + 1) * SLOTS], low[here], 1, 0)
    sum_ref[...] += total


def pair_backward(heads, pair, grads, stats, center, spread):
    count, length, _, channels = pair.shape
    rows = 16
    small = pl.BlockSpec((1, rows, SLOTS, length), lambda n, i: (n, i, 0, 0))
    large = pl.BlockSpec((1, rows, length, channels), lambda n, i: (n, i, 0, 0))
    return pl.pallas_call(
        lambda *refs: pair_backward_kernel(heads, *refs),
        grid=(count, length // rows),
        in_specs=[
            large,
            small,
            small,
            pl.BlockSpec(center.shape, lambda n, i: (0, 0)),
            pl.BlockSpec(spread.shape, lambda n, i: (0, 0)),
        ],
        out_specs=[large, pl.BlockSpec((SLOTS, channels), lambda n, i: (0, 0))],
        out_shape=[
            jax.ShapeDtypeStruct(pair.shape, BF16),
            jax.ShapeDtypeStruct((SLOTS, channels), F32),
        ],
        compiler_params=pltpu.CompilerParams(vmem_limit_bytes=VMEM_BYTES),
        cost_estimate=pl.CostEstimate(
            flops=2 * pair.size * 4 * 256, bytes_accessed=4 * pair.size, transcendentals=0
        ),
        name="pair_backward",
    )(pair, grads, stats, center, spread)


def split_pair(values, low_half):
    zero = jnp.zeros_like(values)
    return jnp.concatenate([jnp.where(low_half, values, zero), jnp.where(low_half, zero, values)], axis=0)


def attention_forward_kernel(scale, qkv_ref, stat_ref, live_ref, probs_ref, mixed_ref):
    length = mixed_ref.shape[1]
    width = mixed_ref.shape[2]
    pair = probs_ref.shape[3]
    low_half = lax.broadcasted_iota(jnp.int32, (length, pair), 1) < pair // 2
    live = live_ref[0] > 0.0
    for p in range(width // pair):
        query, key, value = (qkv_ref[0, :, s * width + p * pair : s * width + (p + 1) * pair] for s in range(3))
        scores = dot(split_pair(query, low_half), key, 1, 1) * scale
        bias = jnp.concatenate(
            [stat_ref[0, pl.ds(2 * p + s, length, stride=SLOTS), :] for s in range(2)], axis=0
        )
        scores = jnp.where(live, scores + bias, -1000000000.0)
        raised = jnp.exp(scores - jnp.max(scores, axis=1, keepdims=True))
        probs = raised / jnp.sum(raised, axis=1, keepdims=True)
        probs_ref[0, p] = probs
        mixed = dot(probs.astype(BF16), value, 1, 0)
        mixed_ref[0, :, p * pair : (p + 1) * pair] = jnp.where(low_half, mixed[:length], mixed[length:]).astype(BF16)


def attention_forward(qkv, stats, live, width, head_size):
    count, length, _ = qkv.shape
    pair = 2 * head_size
    pairs = width // pair
    return pl.pallas_call(
        lambda *refs: attention_forward_kernel(1.0 / math.sqrt(head_size), *refs),
        grid=(count,),
        in_specs=[
            pl.BlockSpec((1, length, 3 * width), lambda n: (n, 0, 0)),
            pl.BlockSpec((1, length * SLOTS, length), lambda n: (n, 0, 0)),
            pl.BlockSpec((1, 1, length), lambda n: (n, 0, 0)),
        ],
        out_specs=[
            pl.BlockSpec((1, pairs, 2 * length, length), lambda n: (n, 0, 0, 0)),
            pl.BlockSpec((1, length, width), lambda n: (n, 0, 0)),
        ],
        out_shape=[
            jax.ShapeDtypeStruct((count, pairs, 2 * length, length), F32),
            jax.ShapeDtypeStruct((count, length, width), BF16),
        ],
        compiler_params=pltpu.CompilerParams(vmem_limit_bytes=VMEM_BYTES),
        cost_estimate=pl.CostEstimate(flops=2 * count * pairs * 4 * length**3, bytes_accessed=6000000, transcendentals=0),
        name="attention_forward",
    )(qkv, stats.reshape(count, length * SLOTS, length), live)


def attention_backward_kernel(scale, qkv_ref, probs_ref, mixed_ref, out_ref, grad_ref):
    length = mixed_ref.shape[1]
    width = mixed_ref.shape[2]
    pair = probs_ref.shape[3]
    low_half = lax.broadcasted_iota(jnp.int32, (length, pair), 1) < pair // 2
    for p in range(width // pair):
        query, key, value = (qkv_ref[0, :, s * width + p * pair : s * width + (p + 1) * pair] for s in range(3))
        mixed = split_pair(mixed_ref[0, :, p * pair : (p + 1) * pair], low_half)
        probs = probs_ref[0, p]
        d_probs = dot(mixed, value, 1, 1)
        d_scores = (probs * (d_probs - jnp.sum(probs * d_probs, axis=1, keepdims=True))).astype(BF16)
        d_query = dot(d_scores, key, 1, 0) * scale
        parts = (
            jnp.where(low_half, d_query[:length], d_query[length:]),
            dot(d_scores, split_pair(query, low_half), 0, 0) * scale,
            dot(probs.astype(BF16), mixed, 0, 0),
        )
        for s in range(3):
            out_ref[0, :, s * width + p * pair : s * width + (p + 1) * pair] = parts[s].astype(BF16)
        wide = d_scores.astype(F32)
        for s in range(2):
            grad_ref[0, pl.ds(2 * p + s, length, stride=SLOTS), :] = wide[s * length : (s + 1) * length]


def attention_backward(qkv, probs, mixed, width, head_size):
    count, length, _ = qkv.shape
    pair = 2 * head_size
    pairs = width // pair
    d_qkv, d_scores = pl.pallas_call(
        lambda *refs: attention_backward_kernel(1.0 / math.sqrt(head_size), *refs),
        grid=(count,),
        in_specs=[
            pl.BlockSpec((1, length, 3 * width), lambda n: (n, 0, 0)),
            pl.BlockSpec((1, pairs, 2 * length, length), lambda n: (n, 0, 0, 0)),
            pl.BlockSpec((1, length, width), lambda n: (n, 0, 0)),
        ],
        out_specs=[
            pl.BlockSpec((1, length, 3 * width), lambda n: (n, 0, 0)),
            pl.BlockSpec((1, length * SLOTS, length), lambda n: (n, 0, 0)),
        ],
        out_shape=[
            jax.ShapeDtypeStruct((count, length, 3 * width), BF16),
            jax.ShapeDtypeStruct((count, length * SLOTS, length), F32),
        ],
        compiler_params=pltpu.CompilerParams(vmem_limit_bytes=VMEM_BYTES),
        cost_estimate=pl.CostEstimate(flops=2 * count * pairs * 8 * length**3, bytes_accessed=8000000, transcendentals=0),
        name="attention_backward",
    )(qkv, probs, mixed)
    return d_qkv, d_scores.reshape(count, length, SLOTS, length)


def normed_parts(values):
    center = values - jnp.mean(values, axis=-1, keepdims=True)
    inverse = lax.rsqrt(jnp.mean(center * center, axis=-1, keepdims=True) + EPS)
    return center * inverse, inverse


def normed_back(grad_hat, normed, inverse):
    return inverse * (
        grad_hat
        - jnp.mean(grad_hat, axis=-1, keepdims=True)
        - normed * jnp.mean(grad_hat * normed, axis=-1, keepdims=True)
    )


def one_hot(ids, size):
    return (lax.broadcasted_iota(jnp.int32, (ids.shape[0], size), 1) == ids[:, None]).astype(BF16)


def look_up(ids_cath, ids_time, cath_table, time_table):
    return dot(one_hot(ids_cath, cath_table.shape[0]), cath_table, 1, 0) + dot(
        one_hot(ids_time, time_table.shape[0]), time_table, 1, 0
    )


def shards(sizes, activations, pair_repr, cotangent, buckets, pad_mask, cath_ids, time_bins, *weights):
    (
        cath_table,
        time_table,
        cond_attn,
        cond_ffn,
        norm_attn,
        norm_ffn,
        pair_gain,
        qkv_weight,
        out_weight,
        pair_weight,
        gateup_weight,
        down_weight,
    ) = weights
    dp_size, fs_size = sizes
    chips = fs_size // 2
    count = activations.shape[0] * activations.shape[1]
    length, width = activations.shape[2:]
    channels = pair_repr.shape[4]
    heads = pair_weight.shape[1]
    head_size = width // heads
    share = width // fs_size
    slice_c = channels // fs_size
    hidden = down_weight.shape[0] * fs_size
    quarter = hidden // 4
    piece = down_weight.shape[0] // 4
    core = lax.axis_index("fsdp") % 2
    side = lax.axis_index("dp") % 2
    same_core = [[2 * g + c for g in range(chips)] for c in range(2)]
    swap_core = [(i, i ^ 1) for i in range(fs_size)]
    swap_side = [(i, i ^ 1) for i in range(dp_size)]

    def by_core(mine, other):
        return jnp.where(core == 0, mine, other), jnp.where(core == 0, other, mine)

    def to_core(values):
        return lax.ppermute(values, "fsdp", swap_core)

    def to_side(values):
        return lax.ppermute(values, "dp", swap_side)

    def by_side(mine, other):
        return jnp.where(side == 0, mine, other), jnp.where(side == 0, other, mine)

    x = activations.reshape(count, length, width).astype(F32)
    pair = pair_repr.reshape(count, length, length, channels)
    dy = cotangent.reshape(count, length, width).astype(F32)
    positions = lax.broadcasted_iota(jnp.int32, (count, length), 1)
    live = (positions < buckets.reshape(count, 1)) & (
        (pad_mask.reshape(count, length) == 1) | (positions == 0)
    )
    live_lane = live.astype(F32).reshape(count, 1, length)
    live_row = live.astype(F32).reshape(count, length, 1)
    ids = jnp.concatenate([cath_ids.reshape(count), time_bins.reshape(count)])

    small = jnp.concatenate(
        [
            norm_attn.astype(F32),
            norm_ffn.astype(F32),
            pair_gain.astype(F32),
            pair_weight.astype(F32).reshape(-1),
            ids.astype(F32),
        ]
    )
    small = lax.all_gather(small, "fsdp", axis=0, tiled=False)
    offsets = [0]
    for size in (share, share, slice_c, slice_c * heads, count, count):
        offsets.append(offsets[-1] + size)
    norm_attn_all, norm_ffn_all, gain_all, pairw_all, group_cath, group_time = (
        small[:, offsets[k] : offsets[k + 1]] for k in range(6)
    )
    norm_attn_all = norm_attn_all.reshape(1, 1, width)
    norm_ffn_all = norm_ffn_all.reshape(1, 1, width)
    gain_all = gain_all.reshape(channels, 1)
    pairw_all = pairw_all.reshape(channels, heads)

    attn_mine = jnp.concatenate([qkv_weight, out_weight], axis=1)
    attn_all = lax.all_gather(attn_mine, "fsdp", axis=0, tiled=True)
    qkv_all = attn_all[:, : 3 * width]
    out_all = attn_all[:, 3 * width :]
    gateup_parts = gateup_weight.reshape(share, 2, fs_size, 4, piece).transpose(3, 0, 1, 2, 4)
    ffn_parts = jnp.concatenate(
        [gateup_parts.reshape(4, share, 2 * quarter), down_weight.reshape(4, piece, width)], axis=2
    )
    ffn_mine = lax.dynamic_index_in_dim(ffn_parts, 2 * side + core, 0, keepdims=False)
    ffn_other = to_core(lax.dynamic_index_in_dim(ffn_parts, 2 * side + 1 - core, 0, keepdims=False))
    ffn_chip = jnp.concatenate(by_core(ffn_mine, ffn_other), axis=0)
    ffn_all = lax.all_gather(ffn_chip, "fsdp", axis=0, tiled=True, axis_index_groups=same_core)
    gateup_all = ffn_all[:, : 2 * quarter]
    down_all = ffn_all[:, 2 * quarter :]

    raw = look_up(
        group_cath.reshape(-1).astype(jnp.int32), group_time.reshape(-1).astype(jnp.int32), cath_table, time_table
    )
    cond_mine = jnp.concatenate([cond_attn, cond_ffn], axis=1)
    terms = dot(jax.nn.silu(raw).astype(BF16), cond_mine, 1, 0)
    mod = lax.all_to_all(terms, "fsdp", 0, 0, tiled=True)
    mod = jnp.sum(mod.reshape(fs_size, count, 6 * width), axis=0)
    shift_attn, scale_attn, gate_attn, shift_ffn, scale_ffn, gate_ffn = (
        mod[:, None, k * width : (k + 1) * width] for k in range(6)
    )

    eye = lax.broadcasted_iota(jnp.int32, (channels, channels), 0) == lax.broadcasted_iota(
        jnp.int32, (channels, channels), 1
    )
    center = (eye.astype(F32) - 1.0 / channels).astype(BF16)
    gained = gain_all * pairw_all
    bias_weight = jnp.pad(gained.astype(BF16), ((0, 0), (0, length - heads)))
    square_weight = jnp.where(
        lax.broadcasted_iota(jnp.int32, (channels, length), 1) == SLOTS - 1, 1.0 / channels, 0.0
    ).astype(BF16)
    stats = pair_forward(pair, center, bias_weight, square_weight)

    attn_hat, attn_inv = normed_parts(x)
    normed_attn = (attn_hat * norm_attn_all * (1.0 + scale_attn) + shift_attn).astype(BF16)
    rows = count * length
    normed_attn_rows = normed_attn.reshape(rows, width)
    qkv = dot(normed_attn_rows, qkv_all, 1, 0).astype(BF16).reshape(count, length, 3 * width)
    probs, mixed = attention_forward(qkv, stats, live_lane, width, head_size)
    mixed_rows = mixed.reshape(rows, width)
    branch_attn = dot(mixed_rows, out_all, 1, 0).reshape(count, length, width)
    after = x + gate_attn * live_row * branch_attn
    ffn_hat, ffn_inv = normed_parts(after)
    normed_ffn = (ffn_hat * norm_ffn_all * (1.0 + scale_ffn) + shift_ffn).astype(BF16).reshape(rows, width)
    d_branch_ffn = (gate_ffn * live_row * dy).astype(BF16).reshape(rows, width)

    def spread_rows(values):
        both = jnp.stack(by_side(values, to_side(values)))
        return jnp.stack(by_core(both, to_core(both))).reshape(4 * rows, width)

    def sum_rows(values):
        parts = values.reshape(2, 2, rows, width)
        keep = lax.dynamic_index_in_dim(parts, core, 0, keepdims=False)
        away = lax.dynamic_index_in_dim(parts, 1 - core, 0, keepdims=False)
        chip = keep + to_core(away.astype(BF16)).astype(F32)
        keep = lax.dynamic_index_in_dim(chip, side, 0, keepdims=False)
        away = lax.dynamic_index_in_dim(chip, 1 - side, 0, keepdims=False)
        return (keep + to_side(away.astype(BF16)).astype(F32)).reshape(count, length, width)

    normed_four = spread_rows(normed_ffn)
    d_branch_four = spread_rows(d_branch_ffn)
    gate_up = dot(normed_four, gateup_all, 1, 0).astype(BF16).astype(F32)
    gate_part = gate_up[:, :quarter]
    up_part = gate_up[:, quarter:]
    sigma = jax.nn.sigmoid(gate_part)
    silu = gate_part * sigma
    hidden_low = (silu * up_part).astype(BF16)
    branch_part = dot(hidden_low, down_all, 1, 0)
    d_hidden = dot(d_branch_four, down_all, 1, 1)
    d_gate_up = jnp.concatenate(
        [d_hidden * up_part * (sigma * (1.0 + gate_part * (1.0 - sigma))), d_hidden * silu], axis=1
    ).astype(BF16)
    d_normed_ffn = sum_rows(dot(d_gate_up, gateup_all, 1, 1))
    branch_ffn = sum_rows(branch_part)
    ffn_grads = jnp.concatenate(
        [
            dot(normed_four, d_gate_up, 0, 0).astype(BF16),
            dot(hidden_low, d_branch_four, 0, 0).astype(BF16),
        ],
        axis=1,
    )
    ffn_grads = lax.psum_scatter(
        ffn_grads, "fsdp", scatter_dimension=0, tiled=True, axis_index_groups=same_core
    )

    block_out = (after + gate_ffn * live_row * branch_ffn).astype(BF16)
    d_gate_ffn = jnp.sum(live_row * branch_ffn * dy, axis=1)
    d_shift_ffn = jnp.sum(d_normed_ffn, axis=1)
    ffn_dot = jnp.sum(d_normed_ffn * ffn_hat, axis=1)
    d_scale_ffn = ffn_dot * norm_ffn_all[0]
    d_norm_ffn = jnp.sum(ffn_dot * (1.0 + scale_ffn[:, 0]), axis=0)
    d_after = dy + normed_back(d_normed_ffn * norm_ffn_all * (1.0 + scale_ffn), ffn_hat, ffn_inv)

    d_branch_attn = (gate_attn * live_row * d_after).astype(BF16).reshape(rows, width)
    d_gate_attn = jnp.sum(live_row * branch_attn * d_after, axis=1)
    d_mixed = dot(d_branch_attn, out_all, 1, 1).astype(BF16).reshape(count, length, width)
    d_qkv, d_scores = attention_backward(qkv, probs, d_mixed, width, head_size)
    d_qkv_rows = d_qkv.reshape(rows, 3 * width)
    attn_grads = jnp.concatenate(
        [
            dot(normed_attn_rows, d_qkv_rows, 0, 0).astype(BF16),
            dot(mixed_rows, d_branch_attn, 0, 0).astype(BF16),
        ],
        axis=1,
    )
    attn_grads = lax.psum_scatter(attn_grads, "fsdp", scatter_dimension=0, tiled=True)
    d_normed_attn = dot(d_qkv_rows, qkv_all, 1, 1).reshape(count, length, width)
    d_shift_attn = jnp.sum(d_normed_attn, axis=1)
    attn_dot = jnp.sum(d_normed_attn * attn_hat, axis=1)
    d_scale_attn = attn_dot * norm_attn_all[0]
    d_norm_attn = jnp.sum(attn_dot * (1.0 + scale_attn[:, 0]), axis=0)
    grad_input = (
        d_after + normed_back(d_normed_attn * norm_attn_all * (1.0 + scale_attn), attn_hat, attn_inv)
    ).astype(BF16)

    spread = gained - jnp.mean(gained, axis=0, keepdims=True)
    spread = jnp.concatenate(
        [
            jnp.pad(spread.T, ((0, SLOTS - heads), (0, 0))),
            jnp.where(
                lax.broadcasted_iota(jnp.int32, (SLOTS, channels), 0) // 2 == heads // 2, 1.0, 0.0
            ),
        ],
        axis=1,
    ).astype(BF16)
    spread = jnp.tile(spread, (length // SLOTS, 1))
    grad_pair, pair_sum = pair_backward(heads, pair, d_scores, stats, center, spread)

    message = jnp.concatenate(
        [
            jnp.concatenate(
                [d_shift_attn, d_scale_attn, d_gate_attn, d_shift_ffn, d_scale_ffn, d_gate_ffn], axis=1
            ).reshape(-1),
            d_norm_attn,
            d_norm_ffn,
            pair_sum[:heads].reshape(-1),
            (ids // 32).astype(F32),
            (ids % 32).astype(F32),
        ]
    ).astype(BF16)
    message = lax.all_gather(message, EVERY, axis=0, tiled=False)
    cut = count * 6 * width
    d_mod = message[:, :cut].reshape(-1, 6 * width)
    rest = message[:, cut:].astype(F32)
    all_ids = (rest[:, -4 * count : -2 * count] * 32.0 + rest[:, -2 * count :]).astype(jnp.int32)
    all_cath = all_ids[:, :count].reshape(-1)
    all_time = all_ids[:, count:].reshape(-1)
    sums = jnp.sum(rest[:, : 2 * width + heads * channels], axis=0)
    me = lax.axis_index("fsdp")
    grad_norm_attn = lax.dynamic_slice_in_dim(sums[:width], me * share, share)
    grad_norm_ffn = lax.dynamic_slice_in_dim(sums[width : 2 * width], me * share, share)
    pair_sums = sums[2 * width :].reshape(heads, channels).T
    grad_pairw = lax.dynamic_slice_in_dim(pair_sums * gain_all, me * slice_c, slice_c)
    grad_gain = lax.dynamic_slice_in_dim(jnp.sum(pair_sums * pairw_all, axis=1), me * slice_c, slice_c)
    raw_all = look_up(all_cath, all_time, cath_table, time_table)
    grad_cond = dot(jax.nn.silu(raw_all).astype(BF16), d_mod, 0, 0)
    sigma_all = jax.nn.sigmoid(raw_all)
    d_cond = dot(d_mod, cond_mine, 1, 1) * (sigma_all * (1.0 + raw_all * (1.0 - sigma_all)))

    def table_grad(all_of, size):
        hot = one_hot(all_of, size).astype(F32)
        return lax.dot_general(hot, d_cond, (((0,), (0,)), ((), ())), precision=lax.Precision.HIGHEST)

    grad_cath = table_grad(all_cath, cath_table.shape[0])
    grad_time = table_grad(all_time, time_table.shape[0])

    def over_dp(values):
        if dp_size == 2:
            return values.astype(F32) + to_side(values).astype(F32)
        return lax.psum(values, "dp").astype(F32)

    attn_grads = over_dp(attn_grads)
    ffn_rows = ffn_grads.reshape(2, share, 2 * quarter + width)
    keep = lax.dynamic_index_in_dim(ffn_rows, core, 0, keepdims=False)
    away = lax.dynamic_index_in_dim(ffn_rows, 1 - core, 0, keepdims=False)
    halves = jnp.stack(by_core(keep, to_core(away)))
    if dp_size == 2:
        fours = jnp.stack(by_side(halves, to_side(halves))).astype(F32)
    else:
        fours = lax.all_gather(halves, "dp", axis=0, tiled=False).astype(F32)
        fours = jnp.sum(fours.reshape((dp_size // 2, 2) + halves.shape), axis=0)
    fours = fours.reshape(4, share, 2 * quarter + width)
    grad_gateup = (
        fours[:, :, : 2 * quarter].reshape(4, share, 2, fs_size, piece).transpose(1, 2, 3, 0, 4).reshape(share, 2 * hidden)
    )
    grad_down = fours[:, :, 2 * quarter :].reshape(4 * piece, width)

    return (
        block_out.reshape(activations.shape),
        grad_input.reshape(activations.shape),
        grad_pair.reshape(pair_repr.shape),
        grad_cath,
        grad_time,
        grad_cond[:, : 3 * width],
        grad_cond[:, 3 * width :],
        grad_norm_attn,
        grad_norm_ffn,
        grad_gain,
        attn_grads[:, : 3 * width],
        attn_grads[:, 3 * width :],
        grad_pairw,
        grad_gateup,
        grad_down,
    )


def solution(mesh):
    chains = ("dp", "fsdp")
    in_specs = (
        P(None, chains, None, None),
        P(None, chains, None, None, None),
        P(None, chains, None, None),
        P(None, chains),
        P(None, chains, None),
        P(None, chains),
        P(None, chains),
        P(None, "fsdp"),
        P(None, "fsdp"),
        P("fsdp", None),
        P("fsdp", None),
        P("fsdp"),
        P("fsdp"),
        P("fsdp"),
        P("fsdp", None),
        P("fsdp", None),
        P("fsdp", None),
        P("fsdp", None),
        P("fsdp", None),
    )
    out_specs = (
        P(None, chains, None, None),
        P(None, chains, None, None),
        P(None, chains, None, None, None),
        P(None, "fsdp"),
        P(None, "fsdp"),
        P("fsdp", None),
        P("fsdp", None),
        P("fsdp"),
        P("fsdp"),
        P("fsdp"),
        P("fsdp", None),
        P("fsdp", None),
        P("fsdp", None),
        P("fsdp", None),
        P("fsdp", None),
    )
    sizes = (mesh.shape["dp"], mesh.shape["fsdp"])
    return jax.shard_map(
        lambda *args: shards(sizes, *args), mesh=mesh, in_specs=in_specs, out_specs=out_specs, check_vma=False
    )
```
